32 devices in a mesh: pass: 8 (over z, x), head: 4 (over y, core).
Axes of the slice: x: 2, y: 2, z: 4, core: 2. Of those that a mesh axis runs over, the one named last changes fastest.
Arguments:
- queries: bfloat16 [3072, 8192], P('pass', 'head'), may hold values from -4.5 to 4.5
- own_kv: bfloat16 [3072, 8, 256], P('pass', 'head'), may hold values from -4.5 to 4.5
- passage_cache: bfloat16 [128, 512, 8, 256], P('pass', None, 'head'), may hold values from -4.5 to 4.5
- out_weight: bfloat16 [8192, 4096], P('head', 'pass'), may hold values from -3.5 to 3.5
- lists: int32 [24, 8], replicated, may hold values from 0 to 127, as said below
- passage_slot: int32 [128], replicated, may hold values from 0 to 127, as said below
- question_slot: int32 [24], replicated, may hold values from 0 to 23, as said below
Outputs:
- attended: bfloat16 [3072, 4096], P('pass', 'head')
The draws below stay inside these ranges and needn't reach their ends.
Inputs may be any that keep to these rules, and one draw needn't show every extreme that they name: Each question lists 8 different passages. The listed passages of the 3 questions at slots d * 3 to d * 3 + 2 are all different, and at most 3 of them have their cache rows in one aligned block of 16 rows; some block holds exactly 3 of them. `passage_slot`: A permutation. `question_slot`: A permutation.
All inputs are finite; a program needn't handle non-finite values.
Results may differ from the reference program's by a relative error of at most 0.014.
Values may be sent and summed in bfloat16 or wider, within the bound.
A program may use at most 192 MiB of HBM per device.

```python
import jax
import jax.numpy as jnp
from jax import lax

H = 64
KVH = 8
HD = 128
DOUT = 4096
LQ = 128
PLEN = 512
TOPP = 8
Q_DEV = 3
PASS_DEV = 16
NQ = 24
NPASS = 128
TOKENS = 3072
GROUP_ROWS = 2048


def request_layout(key):
    shard_count = NPASS // PASS_DEV
    device_count = NQ // Q_DEV
    entries = Q_DEV * TOPP
    question_slot = jax.random.permutation(jax.random.fold_in(key, 101), NQ).astype(jnp.int32)
    passage_slot = jax.random.permutation(jax.random.fold_in(key, 102), NPASS).astype(jnp.int32)

    def shuffle(subkey):
        return jax.random.permutation(subkey, shard_count).astype(jnp.int32)
    orders = jax.vmap(shuffle)(jax.random.split(jax.random.fold_in(key, 103), device_count))
    first = jax.random.randint(jax.random.fold_in(key, 104), (device_count, shard_count), 0, PASS_DEV)
    second = jax.random.randint(jax.random.fold_in(key, 105), (device_count, shard_count), 0, PASS_DEV)
    base = jnp.minimum(first, second).astype(jnp.int32)
    position = jnp.arange(entries, dtype=jnp.int32) % shard_count
    layer = jnp.arange(entries, dtype=jnp.int32) // shard_count
    shard = orders[:, position]
    local_row = (base[:, position] + layer[None, :]) % PASS_DEV
    cache_row = shard * PASS_DEV + local_row
    passage_of_row = jnp.zeros((NPASS,), jnp.int32).at[passage_slot].set(jnp.arange(NPASS, dtype=jnp.int32))
    by_slot = passage_of_row[cache_row].reshape(NQ, TOPP)
    lists = by_slot[question_slot]
    return (question_slot, passage_slot, lists)


def draw_lists(key, part):
    return request_layout(key)[2]


def draw_passage_slot(key, part):
    return request_layout(key)[1]


def draw_question_slot(key, part):
    return request_layout(key)[0]


def draw_queries(key, part):
    shape = (TOKENS, H, HD)
    values = jnp.clip(jax.random.normal(key, shape, jnp.float32), -4.5, 4.5)
    return values.reshape(TOKENS, H * HD).astype(jnp.bfloat16)


def draw_own_kv(key, part):
    shape = (TOKENS, KVH, 2 * HD)
    values = jnp.clip(jax.random.normal(key, shape, jnp.float32), -4.5, 4.5)
    return values.astype(jnp.bfloat16)


def draw_passage_cache(key, part):
    shape = (NPASS, PLEN, KVH, 2 * HD)
    values = jnp.clip(jax.random.normal(key, shape, jnp.float32), -4.5, 4.5)
    return values.astype(jnp.bfloat16)


def level_of(key, dims, cuts, least, top_value):
    def one(dim, blocks):
        draws = jax.random.uniform(jax.random.fold_in(jax.random.fold_in(key, 6), dim), (blocks,), jnp.float32, least / len(cuts), top_value / len(cuts))
        return jnp.repeat(jnp.exp(draws), dims[dim] // blocks).reshape((-1,) + (1,) * (len(dims) - dim - 1))

    factor_of = one(*cuts[0])
    for cut in cuts[1:]:
        factor_of = factor_of * one(*cut)
    return factor_of


def normal_values(own_key, shape, deviation, limit, pieces=(), kind=jnp.bfloat16):
    level = level_of(own_key, shape, pieces, -0.22, 0.18) if pieces else 1.0
    values = jax.random.normal(own_key, shape, jnp.float32) * deviation * level
    return jnp.minimum(jnp.maximum(values, -limit), limit).astype(kind)


def setup_inputs(seed: int = 0) -> dict:
    streams_of = jax.random.split(jax.random.key(seed), 8)
    queries = draw_queries(jax.random.fold_in(streams_of[7], 71), 0)
    own_kv = draw_own_kv(jax.random.fold_in(streams_of[7], 71), 0)
    passage_cache = draw_passage_cache(jax.random.fold_in(streams_of[7], 71), 0)
    out_weight = normal_values(streams_of[3], (H * HD, DOUT), (20.0 / (H * HD) ** 0.5), 3.5, ((0, 4), (1, 8)))
    lists = draw_lists(jax.random.fold_in(streams_of[7], 71), 0)
    passage_slot = draw_passage_slot(jax.random.fold_in(streams_of[7], 71), 0)
    question_slot = draw_question_slot(jax.random.fold_in(streams_of[7], 71), 0)
    return dict(queries=queries, own_kv=own_kv, passage_cache=passage_cache, out_weight=out_weight, lists=lists, passage_slot=passage_slot, question_slot=question_slot)


def attend(query, keys, values, causal):
    heads = query.shape[1]
    rows = query.shape[0] * heads
    flat = query.reshape(rows, query.shape[2])
    scores = lax.dot_general(flat, keys, (((1,), (1,)), ((), ())), preferred_element_type=jnp.float32)
    scores = scores * (query.shape[2] ** -0.5)
    if causal:
        token = lax.broadcasted_iota(jnp.int32, scores.shape, 0) // heads
        column = lax.broadcasted_iota(jnp.int32, scores.shape, 1)
        scores = jnp.where(column <= token, scores, -1e30)
    row_max = jnp.max(scores, axis=1, keepdims=True)
    weights = jnp.exp(scores - row_max)
    row_total = jnp.sum(weights, axis=1, keepdims=True)
    mixed = jnp.dot(weights.astype(jnp.bfloat16), values, preferred_element_type=jnp.float32) / row_total
    level = row_max + jnp.log(row_total)
    return mixed.astype(jnp.bfloat16).reshape(query.shape[0], heads * query.shape[2]), level.reshape(query.shape[0], heads)


def combine(outputs, levels, heads):
    stacked = jnp.stack(outputs)
    level_stack = jnp.stack(levels)
    peak = jnp.max(level_stack, axis=0, keepdims=True)
    overall = peak + jnp.log(jnp.sum(jnp.exp(level_stack - peak), axis=0, keepdims=True))
    share = jnp.exp(level_stack - overall)
    shaped = stacked.reshape(stacked.shape[0], stacked.shape[1], heads, -1).astype(jnp.float32)
    context = jnp.sum(shaped * share[..., None], axis=0)
    return context.reshape(stacked.shape[1], -1).astype(jnp.bfloat16)


def reference(queries, own_kv, passage_cache, out_weight, lists, passage_slot, question_slot):
    group = H // KVH
    slots = jnp.arange(NQ, dtype=jnp.int32)
    holder = (question_slot[None, :] == slots[:, None]).astype(jnp.int32)
    chosen = jnp.sum(holder[:, :, None] * lists[None, :, :], axis=1).astype(jnp.int32)
    catalog = jnp.arange(NPASS, dtype=jnp.int32)
    picked = (chosen[:, :, None] == catalog[None, None, :]).astype(jnp.int32)
    cache_rows = jnp.sum(picked * passage_slot[None, None, :], axis=2).astype(jnp.int32)
    blocks = queries.reshape(NQ, LQ, KVH, group, HD)
    own_blocks = own_kv.reshape(NQ, LQ, KVH, 2 * HD)

    def per_slot(item):
        query_block, own_block, row_list = item
        head_contexts = []
        for head in range(KVH):
            outputs, levels = [], []
            for index in range(TOPP):
                cache_block = lax.dynamic_index_in_dim(passage_cache, row_list[index], 0, keepdims=False)[:, head]
                mixed, level = attend(query_block[:, head], cache_block[:, :HD], cache_block[:, HD:], False)
                outputs.append(mixed)
                levels.append(level)
            mixed, level = attend(query_block[:, head], own_block[:, head, :HD], own_block[:, head, HD:], True)
            outputs.append(mixed)
            levels.append(level)
            head_contexts.append(combine(outputs, levels, group))
        return jnp.concatenate(head_contexts, axis=1)

    context = lax.map(per_slot, (blocks, own_blocks, cache_rows)).reshape(TOKENS, H * HD)
    result = jnp.zeros((TOKENS, DOUT), jnp.float32)
    for index in range(H * HD // GROUP_ROWS):
        lower = index * GROUP_ROWS
        piece = jnp.dot(context[:, lower:lower + GROUP_ROWS], out_weight[lower:lower + GROUP_ROWS], preferred_element_type=jnp.float32)
        rounded = lax.optimization_barrier(piece.astype(jnp.bfloat16))
        result = result + rounded.astype(jnp.float32)
    return result.astype(jnp.bfloat16)
```

```python
import functools
import math

import jax
import jax.numpy as jnp
from jax import lax
from jax.experimental import pallas as pl
from jax.experimental.pallas import tpu as pltpu
from jax.sharding import PartitionSpec as P

H = 64
KVH = 8
HD = 128
LQ = 128
GROUP = H // KVH
COEF = HD ** (-0.5) * math.log2(math.e)
NEG = -1e30
ROWS = 256


def round_of(a, b, n):
    if n & (n - 1) == 0:
        return a ^ b
    return lax.rem(b - a + n, n)


def pairs_of(k, n):
    if n & (n - 1) == 0:
        return [(p, p ^ k) for p in range(n)]
    return [(p, (p + k) % n) for p in range(n)]


def order_of(n):
    rest = range(1, n)
    return sorted(rest, key=lambda k: (bin(k).count("1"), k))


def gather_kernel(n, most, per_device, order, lists_ref, pslot_ref, qslot_ref, cache_ref, *refs):
    recv_ref, own_row_ref = refs[0], refs[1]
    outs = refs[2 : 2 + len(order)]
    send_row, send_cnt, recv_cnt, buf, in_sem, out_sem = refs[2 + len(order) :]
    me = lax.axis_index("pass")
    pass_dev = cache_ref.shape[0]
    topp, nq = lists_ref.shape
    for k in range(n):
        send_cnt[k] = 0
        recv_cnt[k] = 0
    for i in range(n * most):
        recv_ref[i] = -1
        send_row[i] = 0

    def question(q, carry):
        slot = qslot_ref[q]
        dest = slot // per_device
        local = slot - dest * per_device
        k_send = round_of(me, dest, n)
        for t in range(topp):
            row = pslot_ref[lists_ref[t, q]]
            owner = row // pass_dev

            @pl.when(owner == me)
            def _():
                count = send_cnt[k_send]
                send_row[k_send * most + count] = row - owner * pass_dev
                send_cnt[k_send] = count + 1

            @pl.when(dest == me)
            def _():
                k = round_of(owner, me, n)
                count = recv_cnt[k]
                recv_ref[k * most + count] = local
                recv_cnt[k] = count + 1

        return carry

    lax.fori_loop(0, nq, question, 0)
    for r in range(most):
        own_row_ref[r] = send_row[r]
    copies = []
    for j, k in enumerate(order):
        for r in range(most):
            i = j * most + r
            get = pltpu.make_async_copy(
                cache_ref.at[send_row[k * most + r]], buf.at[i], in_sem.at[i]
            )
            get.start()
            copies.append((get, pltpu.make_async_copy(buf.at[i], outs[j].at[r], out_sem.at[i])))
    for get, put in copies:
        get.wait()
        put.start()
    for get, put in copies:
        put.wait()


def gather(lists, passage_slot, question_slot, cache, n, most, per_device, order):
    item = cache.shape[1:]
    slots = (n - 1) * most
    smem = pl.BlockSpec(memory_space=pltpu.SMEM)
    anyspace = pl.BlockSpec(memory_space=pl.ANY)
    return pl.pallas_call(
        functools.partial(gather_kernel, n, most, per_device, order),
        out_shape=[
            jax.ShapeDtypeStruct((n * most,), jnp.int32),
            jax.ShapeDtypeStruct((most,), jnp.int32),
        ]
        + [jax.ShapeDtypeStruct((most,) + item, cache.dtype)] * len(order),
        in_specs=[smem, smem, smem, anyspace],
        out_specs=[smem, smem] + [anyspace] * len(order),
        scratch_shapes=[
            pltpu.SMEM((n * most,), jnp.int32),
            pltpu.SMEM((n,), jnp.int32),
            pltpu.SMEM((n,), jnp.int32),
            pltpu.VMEM((slots,) + item, cache.dtype),
            pltpu.SemaphoreType.DMA((slots,)),
            pltpu.SemaphoreType.DMA((slots,)),
        ],
        name="gather_items",
        cost_estimate=pl.CostEstimate(
            flops=0, bytes_accessed=2 * slots * math.prod(item) * 2, transcendentals=0
        ),
    )(lists.T, passage_slot, question_slot, cache)


def block_step(q_ref, m_ref, l_ref, acc_ref, question, head, keys, values, causal):
    rows = q_ref.shape[2]
    step = min(ROWS, rows)
    width = keys.shape[0]
    ones = jnp.ones(values.shape, values.dtype)
    extended = jnp.concatenate([values, ones], axis=1)
    for start in range(0, rows, step):
        part = pl.ds(start, step)
        q = q_ref[question, head, part, :]
        scores = (
            lax.dot_general(q, keys, (((1,), (1,)), ((), ())), preferred_element_type=jnp.float32)
            * COEF
        )
        if causal:
            token = lax.broadcasted_iota(jnp.int32, scores.shape, 0) % LQ
            column = lax.broadcasted_iota(jnp.int32, scores.shape, 1)
            scores = jnp.where(column <= token, scores, NEG)
        old = m_ref[question, head, part, :]
        new = jnp.maximum(old, jnp.max(scores, axis=1, keepdims=True))
        weights = jnp.exp2(scores - jnp.concatenate([new] * (width // HD), axis=1))
        mixed = jnp.dot(
            weights.astype(jnp.bfloat16), extended, preferred_element_type=jnp.float32
        )
        alpha = jnp.exp2(old - new)
        m_ref[question, head, part, :] = new
        l_ref[question, head, part, :] = l_ref[question, head, part, :] * alpha + mixed[:, HD:]
        acc_ref[question, head, part, :] = (
            acc_ref[question, head, part, :] * alpha + mixed[:, :HD]
        )


def attend_kernel(first, last, rounds, most, *refs):
    refs = list(refs)
    recv_ref, q_ref = refs.pop(0), refs.pop(0)
    if first:
        row_ref, own_ref, cache_ref = refs.pop(0), refs.pop(0), refs.pop(0)
        sources = None
        entries = most
    else:
        state_in = [refs.pop(0) for _ in range(3)]
        sources = [refs.pop(0) for _ in rounds]
        entries = len(rounds) * most
    if last:
        out_ref = refs.pop(0)
        m_ref, l_ref, acc_ref = [refs.pop(0) for _ in range(3)]
    else:
        m_ref, l_ref, acc_ref = [refs.pop(0) for _ in range(3)]
    buf, sem = refs
    per_device, heads = q_ref.shape[0], q_ref.shape[1]

    def fetch(i, slot):
        if first:
            pltpu.make_async_copy(cache_ref.at[row_ref[i]], buf.at[slot], sem.at[slot]).start()
            return
        for j in range(len(rounds)):

            @pl.when(i // most == j)
            def _():
                pltpu.make_async_copy(
                    sources[j].at[i - j * most], buf.at[slot], sem.at[slot]
                ).start()

    def tag_of(i):
        if first:
            return recv_ref[i]
        k = jnp.int32(0)
        for j, value in enumerate(rounds):
            k = jnp.where(i // most == j, value, k)
        return recv_ref[k * most + lax.rem(i, most)]

    fetch(jnp.int32(0), 0)
    if first:
        m_ref[...] = jnp.full(m_ref.shape, NEG, jnp.float32)
        l_ref[...] = jnp.zeros(l_ref.shape, jnp.float32)
        acc_ref[...] = jnp.zeros(acc_ref.shape, jnp.float32)

        def own_block(question, carry):
            for head in range(heads):
                block = own_ref[question, head]
                block_step(
                    q_ref, m_ref, l_ref, acc_ref, question, head, block[:, :HD], block[:, HD:], True
                )
            return carry

        lax.fori_loop(0, per_device, own_block, 0)
    else:
        m_ref[...] = state_in[0][...]
        l_ref[...] = state_in[1][...]
        acc_ref[...] = state_in[2][...]

    def item(i, carry):
        slot = lax.rem(i, 2)
        pltpu.make_async_copy(buf.at[slot], buf.at[slot], sem.at[slot]).wait()

        @pl.when(i + 1 < entries)
        def _():
            fetch(i + 1, lax.rem(i + 1, 2))

        tag = tag_of(i)

        @pl.when(tag >= 0)
        def _():
            for head in range(heads):
                block_step(
                    q_ref,
                    m_ref,
                    l_ref,
                    acc_ref,
                    tag,
                    head,
                    buf[slot, head, :, :HD],
                    buf[slot, head, :, HD:],
                    False,
                )

        return carry

    lax.fori_loop(0, entries, item, 0)
    if last:
        for question in range(per_device):
            for head in range(heads):
                for g in range(GROUP):
                    part = pl.ds(g * LQ, LQ)
                    column = (head * GROUP + g) * HD
                    out_ref[pl.ds(question * LQ, LQ), pl.ds(column, HD)] = (
                        acc_ref[question, head, part, :] / l_ref[question, head, part, :]
                    ).astype(out_ref.dtype)


def attend_call(first, last, rounds, most, recv, q, rest, item):
    per_device, heads, rows, _ = q.shape
    state = jax.ShapeDtypeStruct(q.shape, jnp.float32)
    smem = pl.BlockSpec(memory_space=pltpu.SMEM)
    vmem = pl.BlockSpec(memory_space=pltpu.VMEM)
    anyspace = pl.BlockSpec(memory_space=pl.ANY)
    if first:
        in_specs = [smem, vmem, smem, vmem, anyspace]
        entries = most
    else:
        in_specs = [smem, vmem] + [vmem] * 3 + [anyspace] * len(rounds)
        entries = most * len(rounds)
    scratch = [pltpu.VMEM((2,) + item, q.dtype), pltpu.SemaphoreType.DMA((2,))]
    if last:
        out_shape = jax.ShapeDtypeStruct((per_device * LQ, heads * GROUP * HD), q.dtype)
        out_specs = vmem
        scratch = [pltpu.VMEM(q.shape, jnp.float32)] * 3 + scratch
    else:
        out_shape = [state] * 3
        out_specs = [vmem] * 3
    weights = entries * heads * rows * item[1]
    return pl.pallas_call(
        functools.partial(attend_kernel, first, last, rounds, most),
        out_shape=out_shape,
        in_specs=in_specs,
        out_specs=out_specs,
        scratch_shapes=scratch,
        name="attend_first" if first else ("attend_last" if last else "attend_more"),
        cost_estimate=pl.CostEstimate(
            flops=weights * HD * 4,
            bytes_accessed=entries * math.prod(item) * 2,
            transcendentals=weights,
        ),
    )(recv, q, *rest)


def body(queries, own_kv, passage_cache, out_weight, lists, passage_slot, question_slot):
    n = lax.axis_size("pass")
    per_device = queries.shape[0] // LQ
    heads = own_kv.shape[1]
    entries = per_device * lists.shape[1]
    most = (entries + n - 1) // n
    order = order_of(n)
    cache = jnp.transpose(passage_cache, (0, 2, 1, 3))
    recv, own_row, *items = gather(
        lists, passage_slot, question_slot, cache, n, most, per_device, order
    )
    arrived = [
        lax.ppermute(item, "pass", pairs_of(k, n)) for k, item in zip(order, items)
    ]
    full_weight = lax.all_gather(out_weight, "pass", axis=1, tiled=True)
    q = (
        queries.reshape(per_device, LQ, heads, GROUP, HD)
        .transpose(0, 2, 3, 1, 4)
        .reshape(per_device, heads, GROUP * LQ, HD)
    )
    own = own_kv.reshape(per_device, LQ, heads, 2 * HD).transpose(0, 2, 1, 3)
    item = cache.shape[1:]
    state = attend_call(True, False, (0,), most, recv, q, (own_row, own, cache), item)
    calls = 3
    bounds = [len(order) * i // calls for i in range(calls + 1)]
    for i in range(calls):
        rounds = tuple(order[bounds[i] : bounds[i + 1]])
        rest = tuple(state) + tuple(arrived[bounds[i] : bounds[i + 1]])
        state = attend_call(False, i == calls - 1, rounds, most, recv, q, rest, item)
    context = state
    partial_value = jnp.dot(context, full_weight, preferred_element_type=jnp.float32)
    return lax.psum_scatter(
        partial_value.astype(jnp.bfloat16), "head", scatter_dimension=1, tiled=True
    )


def solution(mesh):
    in_specs = (
        P("pass", "head"),
        P("pass", "head", None),
        P("pass", None, "head", None),
        P("head", "pass"),
        P(),
        P(),
        P(),
    )
    out_specs = P("pass", "head")
    return jax.shard_map(body, mesh=mesh, in_specs=in_specs, out_specs=out_specs, check_vma=False)
```

```python
import functools
import math

import jax
import jax.numpy as jnp
from jax import lax
from jax.experimental import pallas as pl
from jax.experimental.pallas import tpu as pltpu
from jax.sharding import PartitionSpec as P

H = 64
KVH = 8
HD = 128
LQ = 128
GROUP = H // KVH
COEF = HD ** (-0.5) * math.log2(math.e)
NEG = -1e30
ROWS = 256


def round_of(a, b, n):
    if n & (n - 1) == 0:
        return a ^ b
    return lax.rem(b - a + n, n)


def pairs_of(k, n):
    if n & (n - 1) == 0:
        return [(p, p ^ k) for p in range(n)]
    return [(p, (p + k) % n) for p in range(n)]


def order_of(n):
    rest = range(1, n)
    return sorted(rest, key=lambda k: (bin(k).count("1"), k))


def gather_kernel(n, most, per_device, order, lists_ref, pslot_ref, qslot_ref, cache_ref, *refs):
    recv_ref, own_row_ref = refs[0], refs[1]
    outs = refs[2 : 2 + len(order)]
    send_row, send_cnt, recv_cnt, buf, in_sem, out_sem = refs[2 + len(order) :]
    me = lax.axis_index("pass")
    pass_dev = cache_ref.shape[0]
    topp, nq = lists_ref.shape
    for k in range(n):
        send_cnt[k] = 0
        recv_cnt[k] = 0
    for i in range(n * most):
        recv_ref[i] = -1
        send_row[i] = 0

    def question(q, carry):
        slot = qslot_ref[q]
        dest = slot // per_device
        local = slot - dest * per_device
        k_send = round_of(me, dest, n)
        for t in range(topp):
            row = pslot_ref[lists_ref[t, q]]
            owner = row // pass_dev

            @pl.when(owner == me)
            def _():
                count = send_cnt[k_send]
                send_row[k_send * most + count] = row - owner * pass_dev
                send_cnt[k_send] = count + 1

            @pl.when(dest == me)
            def _():
                k = round_of(owner, me, n)
                count = recv_cnt[k]
                recv_ref[k * most + count] = local
                recv_cnt[k] = count + 1

        return carry

    lax.fori_loop(0, nq, question, 0)
    for r in range(most):
        own_row_ref[r] = send_row[r]
    copies = []
    for j, k in enumerate(order):
        for r in range(most):
            i = j * most + r
            get = pltpu.make_async_copy(
                cache_ref.at[send_row[k * most + r]], buf.at[i], in_sem.at[i]
            )
            get.start()
            copies.append((get, pltpu.make_async_copy(buf.at[i], outs[j].at[r], out_sem.at[i])))
    for get, put in copies:
        get.wait()
        put.start()
    for get, put in copies:
        put.wait()


def gather(lists, passage_slot, question_slot, cache, n, most, per_device, order):
    item = cache.shape[1:]
    slots = (n - 1) * most
    smem = pl.BlockSpec(memory_space=pltpu.SMEM)
    anyspace = pl.BlockSpec(memory_space=pl.ANY)
    return pl.pallas_call(
        functools.partial(gather_kernel, n, most, per_device, order),
        out_shape=[
            jax.ShapeDtypeStruct((n * most,), jnp.int32),
            jax.ShapeDtypeStruct((most,), jnp.int32),
        ]
        + [jax.ShapeDtypeStruct((most,) + item, cache.dtype)] * len(order),
        in_specs=[smem, smem, smem, anyspace],
        out_specs=[smem, smem] + [anyspace] * len(order),
        scratch_shapes=[
            pltpu.SMEM((n * most,), jnp.int32),
            pltpu.SMEM((n,), jnp.int32),
            pltpu.SMEM((n,), jnp.int32),
            pltpu.VMEM((slots,) + item, cache.dtype),
            pltpu.SemaphoreType.DMA((slots,)),
            pltpu.SemaphoreType.DMA((slots,)),
        ],
        name="gather_items",
        cost_estimate=pl.CostEstimate(
            flops=0, bytes_accessed=2 * slots * math.prod(item) * 2, transcendentals=0
        ),
    )(lists.T, passage_slot, question_slot, cache)


def block_step(q_ref, m_ref, l_ref, acc_ref, question, head, keys, values, causal):
    rows = q_ref.shape[2]
    step = min(ROWS, rows)
    width = keys.shape[0]
    ones = jnp.ones(values.shape, values.dtype)
    extended = jnp.concatenate([values, ones], axis=1)
    for start in range(0, rows, step):
        part = pl.ds(start, step)
        q = q_ref[question, head, part, :]
        scores = (
            lax.dot_general(q, keys, (((1,), (1,)), ((), ())), preferred_element_type=jnp.float32)
            * COEF
        )
        if causal:
            token = lax.broadcasted_iota(jnp.int32, scores.shape, 0) % LQ
            column = lax.broadcasted_iota(jnp.int32, scores.shape, 1)
            scores = jnp.where(column <= token, scores, NEG)
        old = m_ref[question, head, part, :]
        new = jnp.maximum(old, jnp.max(scores, axis=1, keepdims=True))
        weights = jnp.exp2(scores - jnp.concatenate([new] * (width // HD), axis=1))
        mixed = jnp.dot(
            weights.astype(jnp.bfloat16), extended, preferred_element_type=jnp.float32
        )
        alpha = jnp.exp2(old - new)
        m_ref[question, head, part, :] = new
        l_ref[question, head, part, :] = l_ref[question, head, part, :] * alpha + mixed[:, HD:]
        acc_ref[question, head, part, :] = (
            acc_ref[question, head, part, :] * alpha + mixed[:, :HD]
        )


def attend_kernel(first, last, rounds, most, *refs):
    refs = list(refs)
    recv_ref, q_ref = refs.pop(0), refs.pop(0)
    if first:
        row_ref, own_ref, cache_ref = refs.pop(0), refs.pop(0), refs.pop(0)
        sources = None
        entries = most
    else:
        state_in = [refs.pop(0) for _ in range(3)]
        sources = [refs.pop(0) for _ in rounds]
        entries = len(rounds) * most
    if last:
        out_ref = refs.pop(0)
        m_ref, l_ref, acc_ref = [refs.pop(0) for _ in range(3)]
    else:
        m_ref, l_ref, acc_ref = [refs.pop(0) for _ in range(3)]
    buf, sem = refs
    per_device, heads = q_ref.shape[0], q_ref.shape[1]

    def fetch(i, slot):
        if first:
            pltpu.make_async_copy(cache_ref.at[row_ref[i]], buf.at[slot], sem.at[slot]).start()
            return
        for j in range(len(rounds)):

            @pl.when(i // most == j)
            def _():
                pltpu.make_async_copy(
                    sources[j].at[i - j * most], buf.at[slot], sem.at[slot]
                ).start()

    def tag_of(i):
        if first:
            return recv_ref[i]
        k = jnp.int32(0)
        for j, value in enumerate(rounds):
            k = jnp.where(i // most == j, value, k)
        return recv_ref[k * most + lax.rem(i, most)]

    fetch(jnp.int32(0), 0)
    if first:
        m_ref[...] = jnp.full(m_ref.shape, NEG, jnp.float32)
        l_ref[...] = jnp.zeros(l_ref.shape, jnp.float32)
        acc_ref[...] = jnp.zeros(acc_ref.shape, jnp.float32)

        def own_block(question, carry):
            for head in range(heads):
                block = own_ref[question, head]
                block_step(
                    q_ref, m_ref, l_ref, acc_ref, question, head, block[:, :HD], block[:, HD:], True
                )
            return carry

        lax.fori_loop(0, per_device, own_block, 0)
    else:
        m_ref[...] = state_in[0][...]
        l_ref[...] = state_in[1][...]
        acc_ref[...] = state_in[2][...]

    def item(i, carry):
        slot = lax.rem(i, 2)
        pltpu.make_async_copy(buf.at[slot], buf.at[slot], sem.at[slot]).wait()

        @pl.when(i + 1 < entries)
        def _():
            fetch(i + 1, lax.rem(i + 1, 2))

        tag = tag_of(i)

        @pl.when(tag >= 0)
        def _():
            for head in range(heads):
                block_step(
                    q_ref,
                    m_ref,
                    l_ref,
                    acc_ref,
                    tag,
                    head,
                    buf[slot, head, :, :HD],
                    buf[slot, head, :, HD:],
                    False,
                )

        return carry

    lax.fori_loop(0, entries, item, 0)
    if last:
        for question in range(per_device):
            for head in range(heads):
                for g in range(GROUP):
                    part = pl.ds(g * LQ, LQ)
                    column = (head * GROUP + g) * HD
                    out_ref[pl.ds(question * LQ, LQ), pl.ds(column, HD)] = (
                        acc_ref[question, head, part, :] / l_ref[question, head, part, :]
                    ).astype(out_ref.dtype)


def attend_call(first, last, rounds, most, recv, q, rest, item):
    per_device, heads, rows, _ = q.shape
    state = jax.ShapeDtypeStruct(q.shape, jnp.float32)
    smem = pl.BlockSpec(memory_space=pltpu.SMEM)
    vmem = pl.BlockSpec(memory_space=pltpu.VMEM)
    anyspace = pl.BlockSpec(memory_space=pl.ANY)
    if first:
        in_specs = [smem, vmem, smem, vmem, anyspace]
        entries = most
    else:
        in_specs = [smem, vmem] + [vmem] * 3 + [anyspace] * len(rounds)
        entries = most * len(rounds)
    scratch = [pltpu.VMEM((2,) + item, q.dtype), pltpu.SemaphoreType.DMA((2,))]
    if last:
        out_shape = jax.ShapeDtypeStruct((per_device * LQ, heads * GROUP * HD), q.dtype)
        out_specs = vmem
        scratch = [pltpu.VMEM(q.shape, jnp.float32)] * 3 + scratch
    else:
        out_shape = [state] * 3
        out_specs = [vmem] * 3
    weights = entries * heads * rows * item[1]
    return pl.pallas_call(
        functools.partial(attend_kernel, first, last, rounds, most),
        out_shape=out_shape,
        in_specs=in_specs,
        out_specs=out_specs,
        scratch_shapes=scratch,
        name="attend_first" if first else ("attend_last" if last else "attend_more"),
        cost_estimate=pl.CostEstimate(
            flops=weights * HD * 4,
            bytes_accessed=entries * math.prod(item) * 2,
            transcendentals=weights,
        ),
    )(recv, q, *rest)


def weight_blocks(own, n):
    if n & (n - 1):
        return [lax.all_gather(own, "pass", axis=1, tiled=True)]
    have = {0: own}
    bit = n // 2
    while bit:
        for k in list(have):
            have[k ^ bit] = lax.ppermute(have[k], "pass", pairs_of(bit, n))
        bit //= 2
    return [have[k] for k in range(n)]


def project(context, weights, n):
    parts = [
        jnp.dot(context, weight, preferred_element_type=jnp.float32).astype(jnp.bfloat16)
        for weight in weights
    ]
    me = lax.axis_index("pass")
    bit = len(parts) // 2
    while bit:
        swap = (me & bit) != 0
        parts = [jnp.where(swap, parts[k ^ bit], parts[k]) for k in range(len(parts))]
        bit //= 2
    return jnp.concatenate(parts, axis=1)


def body(queries, own_kv, passage_cache, out_weight, lists, passage_slot, question_slot):
    n = lax.axis_size("pass")
    per_device = queries.shape[0] // LQ
    heads = own_kv.shape[1]
    entries = per_device * lists.shape[1]
    most = (entries + n - 1) // n
    order = order_of(n)
    cache = jnp.transpose(passage_cache, (0, 2, 1, 3))
    recv, own_row, *items = gather(
        lists, passage_slot, question_slot, cache, n, most, per_device, order
    )
    arrived = [
        lax.ppermute(item, "pass", pairs_of(k, n)) for k, item in zip(order, items)
    ]
    weights = weight_blocks(out_weight, n)
    q = (
        queries.reshape(per_device, LQ, heads, GROUP, HD)
        .transpose(0, 2, 3, 1, 4)
        .reshape(per_device, heads, GROUP * LQ, HD)
    )
    own = own_kv.reshape(per_device, LQ, heads, 2 * HD).transpose(0, 2, 1, 3)
    item = cache.shape[1:]
    state = attend_call(True, False, (0,), most, recv, q, (own_row, own, cache), item)
    calls = 3
    bounds = [len(order) * i // calls for i in range(calls + 1)]
    for i in range(calls):
        rounds = tuple(order[bounds[i] : bounds[i + 1]])
        rest = tuple(state) + tuple(arrived[bounds[i] : bounds[i + 1]])
        state = attend_call(False, i == calls - 1, rounds, most, recv, q, rest, item)
    context = state
    return lax.psum_scatter(
        project(context, weights, n), "head", scatter_dimension=1, tiled=True
    )


def solution(mesh):
    in_specs = (
        P("pass", "head"),
        P("pass", "head", None),
        P("pass", None, "head", None),
        P("head", "pass"),
        P(),
        P(),
        P(),
    )
    out_specs = P("pass", "head")
    return jax.shard_map(body, mesh=mesh, in_specs=in_specs, out_specs=out_specs, check_vma=False)
```
